256 devices in a mesh: ctx: 64 (over z, x, core), head: 4 (over y).
Axes of the slice: x: 4, y: 4, z: 8, core: 2. Of those that a mesh axis runs over, the one named last changes fastest.
Arguments:
- asking_vectors: bfloat16 [32768, 2048], P('ctx', 'head'), may hold values from -6 to 6
- lookup_vectors: bfloat16 [32768, 2048], P('ctx', 'head'), may hold values from -16 to 16
- payload_vectors: bfloat16 [32768, 2048], P('ctx', 'head'), may hold values from -16 to 16
- segment_owner_ids: int32 [128], P('ctx'), may hold values from 0 to 31, never falling along the last dimension, each value on 1 to 12 neighbouring positions
- attender_logit_factor: float32 [16], P('head'), may hold values from 4 to 16
- tier_logit_shift: float32 [16], P('head'), may hold values from -0.2 to 0.4
- final_projection_weights: bfloat16 [2048, 4096], P('head'), may hold values from -0.125 to 0.125
Outputs:
- mixed: bfloat16 [32768, 4096], P('ctx', 'head')
The draws below stay inside these ranges and needn't reach their ends.
All inputs are finite; a program needn't handle non-finite values.
Results may differ from the reference program's by a relative error of at most 0.011.
Values may be sent and summed in bfloat16 or wider, within the bound.
No kernel may reach another device: no remote copies, remote signals or barrier semaphores. Data moves between devices by JAX's collectives and lax.ppermute only.
A program may use at most 64 MiB of HBM per device.

```python
import math
import jax
import jax.numpy as jnp
import numpy as np
from jax import lax

D = 4096
SHARD_ATTENDERS = 16
ATTN_DIMENSION = 128
BLOCK = 256
HEADS_DEV = 4
TOKENS = 32768
NB = 128
FAR = 6
N_HEAD = 4


def layered(key, salt, columns, ratio):
    seeded = jax.random.fold_in(key, salt)
    scales = TOKENS.bit_length() - 1
    summed = jnp.zeros((TOKENS, columns), jnp.float32)
    stretch = 1
    power_sum = 0.0
    for layer in range(scales):
        layer_key = jax.random.fold_in(seeded, layer)
        factor = ratio ** layer
        power_sum = power_sum + factor * factor
        pieces = jax.random.truncated_normal(layer_key, -3.0, 3.0, (TOKENS // stretch, columns), jnp.float32)
        spread = jnp.broadcast_to(pieces[:, None, :], (TOKENS // stretch, stretch, columns))
        summed = summed + factor * spread.reshape(TOKENS, columns)
        stretch = stretch * 2
    return summed / math.sqrt(power_sum)


def shared_direction(key):
    return jax.random.rademacher(jax.random.fold_in(key, 501), (SHARD_ATTENDERS * ATTN_DIMENSION,), jnp.float32)


def shared_level(key):
    coefficient = layered(key, 37, SHARD_ATTENDERS, 0.9)
    return jnp.repeat(coefficient, ATTN_DIMENSION, axis=1)


def key_rest(key):
    rest = layered(key, 11, SHARD_ATTENDERS * ATTN_DIMENSION, 0.9)
    return rest


def draw_lookup_vectors(key, part):
    direction = shared_direction(key)
    summed = 1.2 * shared_level(key) * direction[None, :] + 0.8 * key_rest(key)
    return jnp.clip(summed, -15.0, 15.0).astype(jnp.bfloat16)


def draw_payload_vectors(key, part):
    direction = shared_direction(key)
    own = layered(key, 23, SHARD_ATTENDERS * ATTN_DIMENSION, 0.9)
    summed = 0.9 * shared_level(key) * direction[None, :] + 0.5 * key_rest(key) + 0.6 * own
    return jnp.clip(summed, -15.0, 15.0).astype(jnp.bfloat16)


def draw_asking_vectors(key, part):
    direction = shared_direction(key)
    columns = SHARD_ATTENDERS * ATTN_DIMENSION
    strength_key = jax.random.fold_in(key, 61)
    noise_key = jax.random.fold_in(key, 67)
    strength = jax.random.truncated_normal(strength_key, -2.5, 2.5, (TOKENS, SHARD_ATTENDERS), jnp.float32)
    noise = jax.random.truncated_normal(noise_key, -3.0, 3.0, (TOKENS, columns), jnp.float32)
    summed = 1.5 * jnp.repeat(strength, ATTN_DIMENSION, axis=1) * direction[None, :] + noise
    return jnp.clip(summed, -6.0, 6.0).astype(jnp.bfloat16)


def shard_levels(rng, shape, cuts, low, largest):
    def one(position, parts):
        heights = jax.random.uniform(jax.random.fold_in(jax.random.fold_in(rng, 6), position), (parts,), jnp.float32, low / len(cuts), largest / len(cuts))
        return jnp.repeat(jnp.exp(heights), shape[position] // parts).reshape((-1,) + (1,) * (len(shape) - position - 1))

    level = one(*cuts[0])
    for cut in cuts[1:]:
        level = level * one(*cut)
    return level


def length_profile(amount, total, bound, lean):
    loads = [(1 << 20) // math.isqrt(grade ** lean) + 1 for grade in range(2, amount + 1)]
    surplus, given = total - bound - (amount - 1), [1] * (amount - 1)
    while surplus > 0:
        candidates = [i for i in range(amount - 1) if given[i] < bound]
        pool, left = sum([loads[i] for i in candidates]), surplus
        for i in candidates:
            more = min(bound - given[i], max(1, left * loads[i] // pool), surplus)
            given[i] = given[i] + more
            surplus = surplus - more
    return np.array([bound] + given)


def ragged(stream_key, count, total, reach, skew):
    if count == 2:
        one = jax.random.randint(stream_key, (), max(1, total - reach), min(reach, total - 1) + 1)
        return jnp.stack([one, total - one])
    sizes = jnp.asarray(length_profile(count, total, reach, skew), jnp.int32)
    pairs = (count - 1) // 2
    giver, taker = sizes[1:1 + 2 * pairs:2], sizes[2:2 + 2 * pairs:2]
    room = jnp.minimum(giver - 1, reach - taker)
    moved = jax.random.randint(jax.random.fold_in(stream_key, 1), (pairs,), 0, 1 << 20) % (room + 1)
    sizes = sizes.at[1:1 + 2 * pairs:2].set(giver - moved).at[2:2 + 2 * pairs:2].set(taker + moved)
    return sizes[jax.random.permutation(jax.random.fold_in(stream_key, 2), count)]


def gaussian(key, shape, scale, bound, cuts=(), held_as=jnp.bfloat16):
    values = jax.random.normal(key, shape, jnp.float32) * scale
    if len(cuts) > 0:
        values = shard_levels(key, shape, cuts, -0.22, 0.18) * values
    return jnp.clip(values, min=-bound, max=bound).astype(held_as)


def setup_inputs(seed: int = 0) -> dict:
    arg_keys = jax.random.split(jax.random.key(seed), 8)
    return {
        "asking_vectors": draw_asking_vectors(jax.random.fold_in(arg_keys[7], 71), 0),
        "lookup_vectors": draw_lookup_vectors(jax.random.fold_in(arg_keys[7], 71), 0),
        "payload_vectors": draw_payload_vectors(jax.random.fold_in(arg_keys[7], 71), 0),
        "segment_owner_ids": jnp.searchsorted(jnp.cumsum(ragged(arg_keys[3], NB // 4, NB, 12, 1)), jnp.arange(NB), side="right").astype(jnp.int32),
        "attender_logit_factor": jnp.clip(jnp.exp(math.log(16.0) - 1.3862944 * jax.random.uniform(arg_keys[4], (SHARD_ATTENDERS,), jnp.float32) ** shard_levels(arg_keys[4], (SHARD_ATTENDERS,), ((0, 4),), -0.2, 0.2)), 4.0, 16.0),
        "tier_logit_shift": jnp.clip(-0.2 + 0.6 * jax.random.uniform(arg_keys[5], (SHARD_ATTENDERS,), jnp.float32) ** shard_levels(arg_keys[5], (SHARD_ATTENDERS,), ((0, 4),), -0.2, 0.2), -0.2, 0.4),
        "final_projection_weights": gaussian(arg_keys[6], (SHARD_ATTENDERS * ATTN_DIMENSION, D), (SHARD_ATTENDERS * ATTN_DIMENSION) ** -0.5, 0.125, ((0, 4),)),
    }


EPS = 1e-06

def unit_rows(matrix):
    return matrix * lax.rsqrt(lax.optimization_barrier(jnp.mean(matrix * matrix, axis=-1, keepdims=True)) + EPS)

def run_means(matrix, attender_dimension):
    shaped = matrix.reshape((matrix.shape[0] // attender_dimension, attender_dimension) + matrix.shape[1:])
    return lax.optimization_barrier(jnp.mean(shaped, axis=1))

def attend(query_rows, key_rows, value_rows, logit_multiplier, offset, keep, numer, denom):
    scores = jnp.einsum('qhd,khd->hqk', query_rows.astype(jnp.float32), key_rows.astype(jnp.float32))
    weights = jnp.exp(scores * logit_multiplier[:, None, None] + offset[:, None, None]) * keep
    denom = denom + jnp.transpose(lax.optimization_barrier(jnp.sum(weights, axis=-1)))
    rounded = lax.optimization_barrier(weights.astype(jnp.bfloat16)).astype(jnp.float32)
    numer = numer + jnp.einsum('hqk,khd->qhd', rounded, value_rows.astype(jnp.float32))
    return (numer, denom)

def reference(asking_vectors, lookup_vectors, payload_vectors, segment_owner_ids, attender_logit_factor, tier_logit_shift, final_projection_weights):
    q_unit = unit_rows(asking_vectors.astype(jnp.float32).reshape(TOKENS, SHARD_ATTENDERS, ATTN_DIMENSION)).astype(jnp.bfloat16)
    k_unit = unit_rows(lookup_vectors.astype(jnp.float32).reshape(TOKENS, SHARD_ATTENDERS, ATTN_DIMENSION))
    k_near = k_unit.astype(jnp.bfloat16)
    v_near = payload_vectors.reshape(TOKENS, SHARD_ATTENDERS, ATTN_DIMENSION)
    v_wide = v_near.astype(jnp.float32)
    logit_multiplier = attender_logit_factor / ATTN_DIMENSION
    coarse_keys = []
    coarse_values = []
    for level in range(1, FAR + 1):
        span = 2 ** level
        coarse_keys.append(run_means(k_unit, span).astype(jnp.bfloat16).reshape(NB // span, BLOCK, SHARD_ATTENDERS, ATTN_DIMENSION))
        coarse_values.append(run_means(v_wide, span).astype(jnp.bfloat16).reshape(NB // span, BLOCK, SHARD_ATTENDERS, ATTN_DIMENSION))

    def one_block(index):
        start = index * BLOCK
        partner = jnp.bitwise_xor(index, 1)
        other = partner * BLOCK
        query_rows = lax.dynamic_slice_in_dim(q_unit, start, BLOCK, 0)
        numer = jnp.zeros((BLOCK, SHARD_ATTENDERS, ATTN_DIMENSION), jnp.float32)
        denom = jnp.zeros((BLOCK, SHARD_ATTENDERS), jnp.float32)
        still = jnp.zeros((SHARD_ATTENDERS,), jnp.float32)
        numer, denom = attend(query_rows, lax.dynamic_slice_in_dim(k_near, start, BLOCK, 0), lax.dynamic_slice_in_dim(v_near, start, BLOCK, 0), logit_multiplier, still, 1.0, numer, denom)
        keep = (segment_owner_ids[index] == segment_owner_ids[partner]).astype(jnp.float32)
        numer, denom = attend(query_rows, lax.dynamic_slice_in_dim(k_near, other, BLOCK, 0), lax.dynamic_slice_in_dim(v_near, other, BLOCK, 0), logit_multiplier, still, keep, numer, denom)
        for level in range(1, FAR + 1):
            node = jnp.bitwise_xor(jnp.right_shift(index, level), 1)
            numer, denom = attend(query_rows, coarse_keys[level - 1][node], coarse_values[level - 1][node], logit_multiplier, -level * tier_logit_shift, 1.0, numer, denom)
        return (numer / denom[:, :, None]).astype(jnp.bfloat16)
    attended = lax.map(one_block, jnp.arange(NB, dtype=jnp.int32)).reshape(TOKENS, SHARD_ATTENDERS * ATTN_DIMENSION)
    group = HEADS_DEV * ATTN_DIMENSION
    mixed = jnp.zeros((TOKENS, D), jnp.float32)
    for member in range(N_HEAD):
        part = jnp.dot(attended[:, member * group:(member + 1) * group], final_projection_weights[member * group:(member + 1) * group], preferred_element_type=jnp.float32)
        mixed = mixed + lax.optimization_barrier(part.astype(jnp.bfloat16)).astype(jnp.float32)
    return mixed.astype(jnp.bfloat16)
```

```python
import functools
import math

import jax
import jax.numpy as jnp
from jax import lax
from jax.experimental import pallas as pl
from jax.experimental.pallas import tpu as pltpu
from jax.sharding import PartitionSpec as P


EPS = 1e-06
HD = 128
LOG2E = math.log2(math.e)
F32 = jnp.float32
BF16 = jnp.bfloat16
GRANT = 12 << 20
PREP_GRANT = 50 << 20
TURNS = (1, 3, 2)
VM = pl.BlockSpec(memory_space=pltpu.VMEM)
HB = pl.BlockSpec(memory_space=pltpu.HBM)
SM = pl.BlockSpec(memory_space=pltpu.SMEM)


def flip(block, mask):
    count = lax.axis_size("ctx")
    return lax.ppermute(block, "ctx", [(i, i ^ mask) for i in range(count)])


def turn(block, shift):
    count = lax.axis_size("head")
    return lax.ppermute(block, "head", [(i, (i + shift) % count) for i in range(count)])


def call(body, outs, specs, scratch=(), flops=0, grant=GRANT):
    return pl.pallas_call(
        body,
        out_shape=outs,
        in_specs=specs,
        out_specs=jax.tree.map(lambda _: VM, outs),
        scratch_shapes=scratch,
        cost_estimate=pl.CostEstimate(flops=flops, bytes_accessed=1 << 20, transcendentals=0),
        compiler_params=pltpu.CompilerParams(vmem_limit_bytes=grant),
    )


def unit(x):
    return x * lax.rsqrt(jnp.mean(x * x, axis=-1, keepdims=True) + EPS)


def prep_body(
    k_hbm, v_hbm, w_hbm, near_ref, v_ref, one_ref, two_ref, three_ref, far_ref, o1, o2, o3,
    kbuf, buf, ksem, vsem, wsem, *, heads,
):
    rows = kbuf.shape[0]
    part = o1.shape[1]
    count = lax.axis_size("head")
    y = lax.axis_index("head")
    c = lax.axis_index("ctx") % 2
    ks, vs, ws = [], [], []
    for h in range(heads):
        cols = slice(h * HD, (h + 1) * HD)
        ks.append(pltpu.make_async_copy(k_hbm.at[:, cols], kbuf.at[:, cols], ksem.at[h]))
        vs.append(pltpu.make_async_copy(v_hbm.at[:, cols], v_ref.at[:, cols], vsem.at[h]))
    for i, (s, out) in enumerate(zip(TURNS, (o1, o2, o3))):
        at = pl.ds(pl.multiple_of((((y + s) % count) * 2 + c) * part, 128), part)
        ws.append(pltpu.make_async_copy(w_hbm.at[:, at], out, wsem.at[i]))
    for h in range(heads):
        ks[h].start()
        vs[h].start()
    for copy in ws:
        copy.start()
    for h in range(heads):
        cols = slice(h * HD, (h + 1) * HD)
        for piece in range(2):
            if piece == 0:
                ks[h].wait()
                x = unit(kbuf[:, cols].astype(F32))
                near_ref[:, cols] = x.astype(BF16)
            else:
                vs[h].wait()
                x = v_ref[:, cols].astype(F32)
            buf[h, piece, 0:rows, :] = x
            n = rows
            scale = 1.0
            at = 0
            for level in range(1, 7):
                n = n // 2
                scale = scale * 0.5
                x = buf[h, piece, pl.ds(0, n, 2), :] + buf[h, piece, pl.ds(1, n, 2), :]
                out = (x * scale).astype(BF16)
                if level == 1:
                    one_ref[piece, :, cols] = out
                elif level == 2:
                    two_ref[piece, :, cols] = out
                elif level == 3:
                    three_ref[piece, :, cols] = out
                else:
                    far_ref[piece, at : at + n, cols] = out
                    at += n
                if level < 6:
                    buf[h, piece, 0:n, :] = x
    for copy in ws:
        copy.wait()


def mixin(qb, pairs):
    acc = None
    for key, val, off in pairs:
        s = lax.dot_general(qb, key, (((1,), (1,)), ((), ())), preferred_element_type=F32)
        if off is not None:
            s = s + off
        p = jnp.exp2(s).astype(BF16)
        aug = jnp.concatenate([val, jnp.ones_like(val)], axis=1)
        o = jnp.dot(p, aug, preferred_element_type=F32)
        acc = o if acc is None else acc + o
    return acc


def near_body(own_ref, fac_ref, sh_ref, q_ref, near_ref, v_ref, one_ref, qs_ref, acc_ref, *, heads):
    rows = q_ref.shape[0]
    half = rows // 2
    bias = jnp.where(own_ref[0] == own_ref[1], 0.0, -1e30).astype(F32)
    for h in range(heads):
        cols = slice(h * HD, (h + 1) * HD)
        wide = slice(2 * h * HD, 2 * (h + 1) * HD)
        q = unit(q_ref[:, cols].astype(F32)) * (fac_ref[h] * (LOG2E / HD))
        qs_ref[:, cols] = q.astype(BF16)
        off = sh_ref[h] * -LOG2E
        for b in range(2):
            own = slice(b * half, (b + 1) * half)
            oth = slice((1 - b) * half, (2 - b) * half)
            qb = qs_ref[own, cols]
            acc_ref[own, wide] = mixin(
                qb,
                [
                    (near_ref[own, cols], v_ref[own, cols], None),
                    (near_ref[oth, cols], v_ref[oth, cols], bias),
                    (one_ref[0, :, cols], one_ref[1, :, cols], off),
                ],
            )


def gather(refs, part, lo, n, cols):
    return jnp.concatenate([r[part, lo : lo + n, cols] for r in refs], axis=0)


def join_body(*refs):
    out_ref = refs[-1]
    at = 0
    for ref in refs[:-1]:
        n = ref.shape[1]
        out_ref[:, at : at + n] = ref[...]
        at += n


def mid_body(sh_ref, qs_ref, acc_ref, a_ref, b_ref, out_ref, *, heads):
    both = (a_ref, b_ref)
    half = qs_ref.shape[0] // 2
    for h in range(heads):
        cols = slice(h * HD, (h + 1) * HD)
        wide = slice(2 * h * HD, 2 * (h + 1) * HD)
        shift = sh_ref[h] * -LOG2E
        pairs = [
            (gather(both, 0, 128 * f, 128, cols), gather(both, 1, 128 * f, 128, cols), (2.0 + f) * shift)
            for f in range(2)
        ]
        for b in range(2):
            own = slice(b * half, (b + 1) * half)
            out_ref[own, wide] = acc_ref[own, wide] + mixin(qs_ref[own, cols], pairs)


def far_body(sh_ref, qs_ref, acc_ref, *refs, block, heads):
    far, both, out_ref = refs[0:6], refs[6:8], refs[8]
    half = qs_ref.shape[0] // 2
    own = slice(block * half, (block + 1) * half)
    for h in range(heads):
        cols = slice(h * HD, (h + 1) * HD)
        shift = sh_ref[h] * -LOG2E
        pairs = []
        for f in range(3):
            rows = [
                jnp.concatenate([gather(far, p, 32 * f, 32, cols), gather(both, p, 256 + 32 * f, 32, cols)], axis=0)
                for p in range(2)
            ]
            pairs.append((rows[0], rows[1], (4.0 + f) * shift))
        got = mixin(qs_ref[own, cols], pairs)
        num = acc_ref[own, 2 * h * HD : (2 * h + 1) * HD] + got[:, 0:HD]
        den = acc_ref[own, (2 * h + 1) * HD : (2 * h + 2) * HD] + got[:, HD:]
        out_ref[:, cols] = (num / den).astype(BF16)


def own_body(w_ref, a_ref, b_ref, out_ref, buf, sem):
    span = buf.shape[1]
    at = pl.multiple_of(lax.axis_index("head") * span, 128)
    copy = pltpu.make_async_copy(w_ref.at[:, pl.ds(at, span)], buf, sem)
    copy.start()
    copy.wait()
    for i, a in enumerate((a_ref, b_ref)):
        n = a.shape[0]
        out_ref[i * n : (i + 1) * n, :] = jnp.dot(a[...], buf[...], preferred_element_type=F32)


def add_body(acc_ref, *refs, terms):
    blocks, ours, theirs, out_ref = refs[: 2 * terms], refs[2 * terms : 3 * terms], refs[3 * terms : 4 * terms], refs[-1]
    width = ours[0].shape[1]
    c = lax.axis_index("ctx") % 2
    for place, ws in ((c, ours), (1 - c, theirs)):
        at = pl.ds(pl.multiple_of(place * width, 128), width)
        for i in range(2):
            n = blocks[0].shape[0]
            rs = slice(i * n, (i + 1) * n)
            acc = acc_ref[rs, at]
            for t, w in enumerate(ws):
                acc += jnp.dot(blocks[2 * t + i][...], w[...], preferred_element_type=F32)
            out_ref[rs, at] = acc.astype(out_ref.dtype)


def per_device(q, k, v, owner, factor, shift, w):
    rows, wide = q.shape
    heads = factor.shape[0]
    S = jax.ShapeDtypeStruct
    nh = lax.axis_size("head")
    span = w.shape[1] // nh
    part = span // 2
    k_rows = w.shape[0]

    near, v_in, one, two, three, far, *slabs = call(
        functools.partial(prep_body, heads=heads),
        [
            S((rows, wide), BF16),
            S((rows, wide), BF16),
            S((2, 256, wide), BF16),
            S((2, 128, wide), BF16),
            S((2, 64, wide), BF16),
            S((2, 56, wide), BF16),
            *[S((k_rows, part), BF16)] * 3,
        ],
        [HB, HB, HB],
        scratch=[
            pltpu.VMEM((rows, wide), BF16),
            pltpu.VMEM((heads, 2, rows, HD), F32),
            pltpu.SemaphoreType.DMA((heads,)),
            pltpu.SemaphoreType.DMA((heads,)),
            pltpu.SemaphoreType.DMA((3,)),
        ],
        grant=PREP_GRANT,
    )(k, v, w)
    send = [turn(b, s) for b, s in zip(slabs, TURNS)]

    f1 = flip(far, 8)
    one_o = flip(one, 1)
    two_x = flip(two, 2)
    three_x2 = flip(three, 4)
    three_x3 = flip(three, 6)

    m5 = jnp.concatenate([far[:, 32:48], f1[:, 32:48]], axis=1)
    m6 = jnp.concatenate([far[:, 48:56], f1[:, 48:56]], axis=1)
    f2 = flip(m5, 16)
    f3 = [flip(m6, 40), flip(m6, 48)]

    qs, acc = call(
        functools.partial(near_body, heads=heads),
        [S((rows, wide), BF16), S((rows, 2 * wide), F32)],
        [SM, SM, SM, VM, VM, VM, VM],
        flops=1 << 30,
    )(owner, factor, shift, q, near, v_in, one_o)

    mine = jnp.concatenate([f1[:, 0:32], f2, *f3], axis=1)
    far_own = [flip(mine, m) for m in (2, 6, 4)]
    held = call(join_body, S((2, 352, wide), BF16), [VM] * 4)(two_x, three_x2, three_x3, mine)
    held_o = flip(held, 1)
    acc = call(
        functools.partial(mid_body, heads=heads),
        S((rows, 2 * wide), F32),
        [SM] + [VM] * 4,
        flops=1 << 29,
    )(shift, qs, acc, held, held_o)

    far_oth = [flip(b, 1) for b in far_own]
    att = []
    for i in range(2):
        att.append(
            call(
                functools.partial(far_body, block=i, heads=heads),
                S((rows // 2, wide), BF16),
                [SM] + [VM] * 10,
                flops=1 << 28,
            )(shift, qs, acc, *far_own, *far_oth, held, held_o)
        )

    left = [turn(a, 1) for a in att]
    right = [turn(a, 3) for a in att]
    across = [turn(left[0], 1), turn(right[1], 3)]

    w_oth = [flip(b, 1) for b in send]
    out = call(
        own_body,
        S((rows, span), F32),
        [HB, VM, VM],
        scratch=[pltpu.VMEM((k_rows, span), BF16), pltpu.SemaphoreType.DMA],
        flops=1 << 29,
    )(pltpu.with_memory_space_constraint(w, pltpu.HBM), *att)
    out = call(
        functools.partial(add_body, terms=2), S((rows, span), F32), [VM] * 9, flops=1 << 30
    )(out, *left, *right, *send[:2], *w_oth[:2])
    return call(
        functools.partial(add_body, terms=1), S((rows, span), BF16), [VM] * 5, flops=1 << 29
    )(out, *across, send[2], w_oth[2])


def solution(mesh):
    placed = (
        P("ctx", "head"),
        P("ctx", "head"),
        P("ctx", "head"),
        P("ctx"),
        P("head"),
        P("head"),
        P("head", None),
    )

    return jax.shard_map(
        per_device, mesh=mesh, in_specs=placed, out_specs=P("ctx", "head"), check_vma=False
    )
```

```python
import functools
import math

import jax
import jax.numpy as jnp
from jax import lax
from jax.experimental import pallas as pl
from jax.experimental.pallas import tpu as pltpu
from jax.sharding import PartitionSpec as P


EPS = 1e-06
HD = 128
LOG2E = math.log2(math.e)
F32 = jnp.float32
BF16 = jnp.bfloat16
GRANT = 12 << 20
PREP_GRANT = 50 << 20
TURNS = (1, 3, 2)
VM = pl.BlockSpec(memory_space=pltpu.VMEM)
HB = pl.BlockSpec(memory_space=pltpu.HBM)
SM = pl.BlockSpec(memory_space=pltpu.SMEM)


def flip(block, mask):
    count = lax.axis_size("ctx")
    return lax.ppermute(block, "ctx", [(i, i ^ mask) for i in range(count)])


def turn(block, shift):
    count = lax.axis_size("head")
    return lax.ppermute(block, "head", [(i, (i + shift) % count) for i in range(count)])


def call(body, outs, specs, scratch=(), flops=0, grant=GRANT, place=None, alias=None):
    return pl.pallas_call(
        body,
        out_shape=outs,
        in_specs=specs,
        out_specs=place or jax.tree.map(lambda _: VM, outs),
        input_output_aliases=alias or {},
        scratch_shapes=scratch,
        cost_estimate=pl.CostEstimate(flops=flops, bytes_accessed=1 << 20, transcendentals=0),
        compiler_params=pltpu.CompilerParams(vmem_limit_bytes=grant),
    )


def unit(x):
    return x * lax.rsqrt(jnp.mean(x * x, axis=-1, keepdims=True) + EPS)


def prep_body(
    k_hbm, v_hbm, w_hbm, near_ref, v_ref, one_ref, two_ref, three_ref, far_ref, o1, o2, o3,
    kbuf, buf, ksem, vsem, wsem, *, heads,
):
    rows = kbuf.shape[0]
    part = o1.shape[1]
    count = lax.axis_size("head")
    y = lax.axis_index("head")
    c = lax.axis_index("ctx") % 2
    ks, vs, ws = [], [], []
    for h in range(heads):
        cols = slice(h * HD, (h + 1) * HD)
        ks.append(pltpu.make_async_copy(k_hbm.at[:, cols], kbuf.at[:, cols], ksem.at[h]))
        vs.append(pltpu.make_async_copy(v_hbm.at[:, cols], v_ref.at[:, cols], vsem.at[h]))
    for i, (s, out) in enumerate(zip(TURNS, (o1, o2, o3))):
        at = pl.ds(pl.multiple_of((((y + s) % count) * 2 + c) * part, 128), part)
        ws.append(pltpu.make_async_copy(w_hbm.at[:, at], out, wsem.at[i]))
    for h in range(heads):
        ks[h].start()
        vs[h].start()
    for copy in ws:
        copy.start()
    for h in range(heads):
        cols = slice(h * HD, (h + 1) * HD)
        for piece in range(2):
            if piece == 0:
                ks[h].wait()
                x = unit(kbuf[:, cols].astype(F32))
                near_ref[:, cols] = x.astype(BF16)
            else:
                vs[h].wait()
                x = v_ref[:, cols].astype(F32)
            buf[h, piece, 0:rows, :] = x
            n = rows
            scale = 1.0
            at = 0
            for level in range(1, 7):
                n = n // 2
                scale = scale * 0.5
                x = buf[h, piece, pl.ds(0, n, 2), :] + buf[h, piece, pl.ds(1, n, 2), :]
                out = (x * scale).astype(BF16)
                if level == 1:
                    one_ref[piece, :, cols] = out
                elif level == 2:
                    two_ref[piece, :, cols] = out
                elif level == 3:
                    three_ref[piece, :, cols] = out
                else:
                    far_ref[piece, at : at + n, cols] = out
                    at += n
                if level < 6:
                    buf[h, piece, 0:n, :] = x
    for copy in ws:
        copy.wait()


def mixin(qb, pairs):
    acc = None
    for key, val, off in pairs:
        s = lax.dot_general(qb, key, (((1,), (1,)), ((), ())), preferred_element_type=F32)
        if off is not None:
            s = s + off
        p = jnp.exp2(s).astype(BF16)
        aug = jnp.concatenate([val, jnp.ones_like(val)], axis=1)
        o = jnp.dot(p, aug, preferred_element_type=F32)
        acc = o if acc is None else acc + o
    return acc


def near_body(own_ref, fac_ref, sh_ref, q_ref, near_ref, v_ref, one_ref, qs_ref, acc_ref, *, heads):
    rows = q_ref.shape[0]
    half = rows // 2
    bias = jnp.where(own_ref[0] == own_ref[1], 0.0, -1e30).astype(F32)
    for h in range(heads):
        cols = slice(h * HD, (h + 1) * HD)
        wide = slice(2 * h * HD, 2 * (h + 1) * HD)
        q = unit(q_ref[:, cols].astype(F32)) * (fac_ref[h] * (LOG2E / HD))
        qs_ref[:, cols] = q.astype(BF16)
        off = sh_ref[h] * -LOG2E
        for b in range(2):
            own = slice(b * half, (b + 1) * half)
            oth = slice((1 - b) * half, (2 - b) * half)
            qb = qs_ref[own, cols]
            acc_ref[own, wide] = mixin(
                qb,
                [
                    (near_ref[own, cols], v_ref[own, cols], None),
                    (near_ref[oth, cols], v_ref[oth, cols], bias),
                    (one_ref[0, :, cols], one_ref[1, :, cols], off),
                ],
            )


def gather(refs, part, lo, n, cols):
    return jnp.concatenate([r[part, lo : lo + n, cols] for r in refs], axis=0)


def join_body(*refs):
    out_ref = refs[-1]
    at = 0
    for ref in refs[:-1]:
        n = ref.shape[1]
        out_ref[:, at : at + n] = ref[...]
        at += n


def mid_body(sh_ref, qs_ref, acc_ref, a_ref, b_ref, out_ref, *, heads):
    both = (a_ref, b_ref)
    half = qs_ref.shape[0] // 2
    for h in range(heads):
        cols = slice(h * HD, (h + 1) * HD)
        wide = slice(2 * h * HD, 2 * (h + 1) * HD)
        shift = sh_ref[h] * -LOG2E
        pairs = [
            (gather(both, 0, 128 * f, 128, cols), gather(both, 1, 128 * f, 128, cols), (2.0 + f) * shift)
            for f in range(2)
        ]
        for b in range(2):
            own = slice(b * half, (b + 1) * half)
            out_ref[own, wide] = acc_ref[own, wide] + mixin(qs_ref[own, cols], pairs)


def far_body(sh_ref, qs_ref, acc_ref, *refs, heads):
    far, outs = refs[0:8], refs[8:10]
    half = qs_ref.shape[0] // 2
    for h in range(heads):
        cols = slice(h * HD, (h + 1) * HD)
        shift = sh_ref[h] * -LOG2E
        pairs = []
        for f in range(3):
            rows = [gather(far, p, 32 * f, 32, cols) for p in range(2)]
            pairs.append((rows[0], rows[1], (4.0 + f) * shift))
        for b in range(2):
            own = slice(b * half, (b + 1) * half)
            got = mixin(qs_ref[own, cols], pairs)
            num = acc_ref[own, 2 * h * HD : (2 * h + 1) * HD] + got[:, 0:HD]
            den = acc_ref[own, (2 * h + 1) * HD : (2 * h + 2) * HD] + got[:, HD:]
            outs[b][:, cols] = (num / den).astype(BF16)


def own_body(w_ref, a_ref, b_ref, out_ref, buf, sem):
    span = buf.shape[1]
    at = pl.multiple_of(lax.axis_index("head") * span, 128)
    copy = pltpu.make_async_copy(w_ref.at[:, pl.ds(at, span)], buf, sem)
    copy.start()
    copy.wait()
    for i, a in enumerate((a_ref, b_ref)):
        n = a.shape[0]
        out_ref[i * n : (i + 1) * n, :] = jnp.dot(a[...], buf[...], preferred_element_type=F32)


def add_body(acc_ref, *refs, terms):
    blocks, ours, theirs, out_ref = refs[: 2 * terms], refs[2 * terms : 3 * terms], refs[3 * terms : 4 * terms], refs[-1]
    width = ours[0].shape[1]
    c = lax.axis_index("ctx") % 2
    for place, ws in ((c, ours), (1 - c, theirs)):
        at = pl.ds(pl.multiple_of(place * width, 128), width)
        for i in range(2):
            n = blocks[0].shape[0]
            rs = slice(i * n, (i + 1) * n)
            acc = acc_ref[rs, at]
            for t, w in enumerate(ws):
                acc += jnp.dot(blocks[2 * t + i][...], w[...], preferred_element_type=F32)
            out_ref[rs, at] = acc.astype(out_ref.dtype)


def last_body(*refs, block):
    acc_ref, a_ref, ours, theirs, out_ref, buf, sem = refs[-7:]
    width = ours.shape[1]
    n = a_ref.shape[0]
    rs = pl.ds(block * n, n)
    c = lax.axis_index("ctx") % 2
    copies = []
    for i, (place, w) in enumerate(((c, ours), (1 - c, theirs))):
        at = pl.ds(pl.multiple_of(place * width, 128), width)
        acc = acc_ref[rs, at] + jnp.dot(a_ref[...], w[...], preferred_element_type=F32)
        buf[i] = acc.astype(BF16)
        copies.append(pltpu.make_async_copy(buf.at[i], out_ref.at[rs, at], sem.at[i]))
        copies[-1].start()
    for copy in copies:
        copy.wait()


def per_device(q, k, v, owner, factor, shift, w):
    rows, wide = q.shape
    heads = factor.shape[0]
    S = jax.ShapeDtypeStruct
    nh = lax.axis_size("head")
    span = w.shape[1] // nh
    part = span // 2
    k_rows = w.shape[0]

    near, v_in, one, two, three, far, *slabs = call(
        functools.partial(prep_body, heads=heads),
        [
            S((rows, wide), BF16),
            S((rows, wide), BF16),
            S((2, 256, wide), BF16),
            S((2, 128, wide), BF16),
            S((2, 64, wide), BF16),
            S((2, 56, wide), BF16),
            *[S((k_rows, part), BF16)] * 3,
        ],
        [HB, HB, HB],
        scratch=[
            pltpu.VMEM((rows, wide), BF16),
            pltpu.VMEM((heads, 2, rows, HD), F32),
            pltpu.SemaphoreType.DMA((heads,)),
            pltpu.SemaphoreType.DMA((heads,)),
            pltpu.SemaphoreType.DMA((3,)),
        ],
        grant=PREP_GRANT,
    )(k, v, w)
    send = [turn(b, s) for b, s in zip(slabs, TURNS)]

    f1 = flip(far, 8)
    one_o = flip(one, 1)
    two_x = flip(two, 2)
    three_x2 = flip(three, 4)
    three_x3 = flip(three, 6)

    m5 = jnp.concatenate([far[:, 32:48], f1[:, 32:48]], axis=1)
    m6 = jnp.concatenate([far[:, 48:56], f1[:, 48:56]], axis=1)
    f2 = flip(m5, 16)
    f3 = [flip(m6, 40), flip(m6, 48)]

    qs, acc = call(
        functools.partial(near_body, heads=heads),
        [S((rows, wide), BF16), S((rows, 2 * wide), F32)],
        [SM, SM, SM, VM, VM, VM, VM],
        flops=1 << 30,
    )(owner, factor, shift, q, near, v_in, one_o)

    mine = jnp.concatenate([f1[:, 0:32], f2, *f3], axis=1)
    far_own = [mine] + [flip(mine, m) for m in (2, 6, 4)]
    held = call(join_body, S((2, 256, wide), BF16), [VM] * 3)(two_x, three_x2, three_x3)
    held_o = flip(held, 1)
    acc = call(
        functools.partial(mid_body, heads=heads),
        S((rows, 2 * wide), F32),
        [SM] + [VM] * 4,
        flops=1 << 29,
    )(shift, qs, acc, held, held_o)

    far_oth = [flip(b, 1) for b in far_own]
    att = call(
        functools.partial(far_body, heads=heads),
        [S((rows // 2, wide), BF16)] * 2,
        [SM] + [VM] * 10,
        flops=1 << 29,
    )(shift, qs, acc, *far_own, *far_oth)

    left = [turn(a, 1) for a in att]
    right = [turn(a, 3) for a in att]
    across = [turn(left[0], 1), turn(right[1], 3)]

    w_oth = [flip(b, 1) for b in send]
    out = call(
        own_body,
        S((rows, span), F32),
        [HB, VM, VM],
        scratch=[pltpu.VMEM((k_rows, span), BF16), pltpu.SemaphoreType.DMA],
        flops=1 << 29,
    )(pltpu.with_memory_space_constraint(w, pltpu.HBM), *att)
    out = call(
        functools.partial(add_body, terms=2), S((rows, span), F32), [VM] * 9, flops=1 << 30
    )(out, *left, *right, *send[:2], *w_oth[:2])
    result = ()
    for i, a in enumerate(across):
        result = (
            call(
                functools.partial(last_body, block=i),
                S((rows, span), BF16),
                [HB] * len(result) + [VM] * 4,
                scratch=[pltpu.VMEM((2, rows // 2, part), BF16), pltpu.SemaphoreType.DMA((2,))],
                flops=1 << 28,
                place=HB,
                alias={0: 0} if result else None,
            )(*result, out, a, send[2], w_oth[2]),
        )
    return result[0]


def solution(mesh):
    placed = (
        P("ctx", "head"),
        P("ctx", "head"),
        P("ctx", "head"),
        P("ctx"),
        P("head"),
        P("head"),
        P("head", None),
    )

    return jax.shard_map(
        per_device, mesh=mesh, in_specs=placed, out_specs=P("ctx", "head"), check_vma=False
    )
```
